32 devices in a mesh: seq: 16 (over z, x, core), tp: 2 (over y).
Axes of the slice: x: 2, y: 2, z: 4, core: 2. Of those that a mesh axis runs over, the one named last changes fastest.
Arguments:
- tokens: bfloat16 [256, 8192], P('tp', 'seq'), may hold values from -6 to 6
- gate_weight: bfloat16 [8192, 14336], P('seq', 'tp'), may hold values from -0.0625 to 0.0625
- up_weight: bfloat16 [8192, 14336], P('seq', 'tp'), may hold values from -0.0625 to 0.0625
- down_weight: bfloat16 [14336, 8192], P('tp', 'seq'), may hold values from -0.09375 to 0.09375
- masks: int32 [2, 112], P(None, 'tp'), may hold values from 0 to 1, as said below
- cotangent: bfloat16 [256, 8192], P('tp', 'seq'), may hold values from -6 to 6
Outputs:
- output: bfloat16 [256, 8192], P('tp', 'seq')
- grad_tokens: bfloat16 [256, 8192], P('tp', 'seq')
- grad_gate: float32 [8192, 14336], P('seq', 'tp')
- grad_up: float32 [8192, 14336], P('seq', 'tp')
- grad_down: float32 [14336, 8192], P('tp', 'seq')
The draws below stay inside these ranges and needn't reach their ends.
Inputs may be any that keep to these rules, and one draw needn't show every extreme that they name: Each row of masks holds exactly 28 ones. Cut a row into 2 groups of 56 consecutive blocks: in every row one group holds exactly 28 ones, and the remaining ones are spread over the other groups as evenly as possible, so that their counts differ by at most one.
All inputs are finite; a program needn't handle non-finite values.
Results may differ from the reference program's by a relative error of at most 0.0049.
Values may be sent and summed in bfloat16 or wider, within the bound.
A program may use at most 192 MiB of HBM per device.

```python
import math
import jax
import jax.numpy as jnp

D = 8192
FF = 14336
BLK = 128
ROWBLK = 128
SEQUENCE_TOKENS = 256
KEEP = 28
N_TP = 2


def draw_masks(key, part):
    block_total = FF // BLK
    kept_total = block_total // 4
    row_blocks = SEQUENCE_TOKENS // ROWBLK
    per_shard = block_total // N_TP
    capacity = 2 * kept_total // N_TP
    remainder = kept_total - capacity
    base_count = remainder // (N_TP - 1)
    extra_count = remainder % (N_TP - 1)

    def one_row(row_key):
        perm_key, selection_key = jax.random.split(row_key)
        order = jax.random.permutation(perm_key, N_TP)
        position = jnp.argsort(order, stable=True).astype(jnp.int32)
        shard_count = jnp.where(position == 0, capacity, base_count + (position - 1 < extra_count).astype(jnp.int32))
        block_rank = jax.vmap(lambda inner_key: jax.random.permutation(inner_key, per_shard))(jax.random.split(selection_key, N_TP))
        chosen = (block_rank < shard_count[:, None]).astype(jnp.int32)
        return chosen.reshape(block_total)
    return jax.vmap(one_row)(jax.random.split(key, row_blocks)).astype(jnp.int32)


def level_of(rng, extent, cuts, least, top_value):
    def one(axis_at, blocks):
        draws = jax.random.uniform(jax.random.fold_in(jax.random.fold_in(rng, 6), axis_at), (blocks,), jnp.float32, least / len(cuts), top_value / len(cuts))
        return jnp.repeat(jnp.exp(draws), extent[axis_at] // blocks).reshape((-1,) + (1,) * (len(extent) - axis_at - 1))

    loudness = one(*cuts[0])
    for cut in cuts[1:]:
        loudness = loudness * one(*cut)
    return loudness


def normal_values(own_key, shape, scale, limit, cuts=(), held_as=jnp.bfloat16):
    drawn = jax.random.normal(own_key, shape, jnp.float32) * scale
    if len(cuts) > 0:
        drawn = level_of(own_key, shape, cuts, -0.22, 0.18) * drawn
    return jnp.clip(drawn, min=-limit, max=limit).astype(held_as)


def setup_inputs(seed: int = 0) -> dict:
    key_of = jax.random.split(jax.random.key(seed), 7)
    tokens = normal_values(key_of[0], (SEQUENCE_TOKENS, D), 1.0, 6.0, ((0, 2), (1, 16)))
    gate_weight = normal_values(key_of[1], (D, FF), D ** -0.5, 0.0625, ((0, 16), (1, 2)))
    up_weight = normal_values(key_of[2], (D, FF), D ** -0.5, 0.0625, ((0, 16), (1, 2)))
    down_weight = normal_values(key_of[3], (FF, D), (KEEP * BLK) ** -0.5, 0.09375, ((0, 2), (1, 16)))
    masks = draw_masks(jax.random.fold_in(key_of[6], 71), 0)
    cotangent = normal_values(key_of[5], (SEQUENCE_TOKENS, D), 1.0, 6.0, ((0, 2), (1, 16)))
    return {"tokens": tokens, "gate_weight": gate_weight, "up_weight": up_weight, "down_weight": down_weight, "masks": masks, "cotangent": cotangent}


def reference(tokens, gate_weight, up_weight, down_weight, masks, cotangent):
    keep = jnp.repeat(jnp.repeat(masks, ROWBLK, axis=0), BLK, axis=1).astype(jnp.float32)
    gate = jnp.dot(tokens, gate_weight, preferred_element_type=jnp.float32)
    up = jnp.dot(tokens, up_weight, preferred_element_type=jnp.float32)
    hidden = (jax.nn.silu(gate) * up * keep).astype(jnp.bfloat16)
    output = jnp.dot(hidden, down_weight, preferred_element_type=jnp.float32).astype(jnp.bfloat16)
    grad_hidden = jnp.dot(cotangent, down_weight.T, preferred_element_type=jnp.float32) * keep
    sigmoid_gate = jax.nn.sigmoid(gate)
    grad_gate_act = (grad_hidden * up * sigmoid_gate * (1.0 + gate * (1.0 - sigmoid_gate))).astype(jnp.bfloat16)
    grad_up_act = (grad_hidden * gate * sigmoid_gate).astype(jnp.bfloat16)
    grad_scale = 1.0 / math.sqrt(SEQUENCE_TOKENS)
    grad_gate = jnp.dot(tokens.T, grad_gate_act, preferred_element_type=jnp.float32) * grad_scale
    grad_up = jnp.dot(tokens.T, grad_up_act, preferred_element_type=jnp.float32) * grad_scale
    grad_down = jnp.dot(hidden.T, cotangent, preferred_element_type=jnp.float32) * grad_scale
    grad_tokens = (jnp.dot(grad_gate_act, gate_weight.T, preferred_element_type=jnp.float32) + jnp.dot(grad_up_act, up_weight.T, preferred_element_type=jnp.float32)).astype(jnp.bfloat16)
    return (output, grad_tokens, grad_gate, grad_up, grad_down)
```

```python
import functools
import math

import jax
import jax.numpy as jnp
from jax import lax
from jax.experimental import pallas as pl
from jax.experimental.pallas import tpu as pltpu
from jax.sharding import PartitionSpec as P

BLK = 128
ROWBLK = 128
KEEP_PART = 4
MESH = pl.DeviceIdType.MESH
VMEM_LIMIT = 60 * 1024 * 1024


def group_of(count):
    for size in (7, 8, 4, 2):
        if count % size == 0:
            return size
    return 1


def tables_kernel(mask_ref, block_ref, live_ref, slot_ref):
    row_blocks, blocks = mask_ref.shape
    capacity = block_ref.shape[1]
    for row in range(row_blocks):
        for slot in range(capacity):
            block_ref[row, slot] = 0
            live_ref[row, slot] = 0

        def step(block, taken, row=row):
            kept = mask_ref[row, block]
            at = jnp.minimum(taken, capacity - 1)
            slot_ref[row, block] = at

            @pl.when(kept == 1)
            def _():
                block_ref[row, at] = block
                live_ref[row, at] = 1

            return taken + kept

        lax.fori_loop(0, blocks, step, jnp.int32(0))


def slot_tables(masks, capacity):
    row_blocks, blocks = masks.shape
    smem = pl.BlockSpec(memory_space=pltpu.SMEM)
    return pl.pallas_call(
        tables_kernel,
        out_shape=(
            jax.ShapeDtypeStruct((row_blocks, capacity), jnp.int32),
            jax.ShapeDtypeStruct((row_blocks, capacity), jnp.int32),
            jax.ShapeDtypeStruct((row_blocks, blocks), jnp.int32),
        ),
        in_specs=[smem],
        out_specs=(smem, smem, smem),
    )(masks)


def rows_kernel(count, tok_ref, cot_ref, tok_all, cot_all, send_sem, recv_sem, own_sem):
    me = lax.axis_index("tp")
    barrier = pltpu.get_barrier_semaphore()
    for shift in range(1, count):
        pl.semaphore_signal(
            barrier, inc=1, device_id={"tp": lax.rem(me + shift, count)}, device_id_type=MESH
        )
    pl.semaphore_wait(barrier, count - 1)
    copies = []
    for which, (src, dst) in enumerate(((tok_ref, tok_all), (cot_ref, cot_all))):
        for shift in range(1, count):
            copy = pltpu.make_async_remote_copy(
                src_ref=src,
                dst_ref=dst.at[me],
                send_sem=send_sem.at[which, shift],
                recv_sem=recv_sem.at[which, shift],
                device_id={"tp": lax.rem(me + shift, count)},
                device_id_type=MESH,
            )
            copy.start()
            copies.append(copy)
        own = pltpu.make_async_copy(src, dst.at[me], own_sem.at[which])
        own.start()
        copies.append(own)
    for copy in copies:
        copy.wait()


def gather_rows(tokens, cotangent):
    count = lax.axis_size("tp")
    rows, feats = tokens.shape
    anywhere = pl.BlockSpec(memory_space=pl.ANY)
    return pl.pallas_call(
        functools.partial(rows_kernel, count),
        out_shape=(jax.ShapeDtypeStruct((count, rows, feats), tokens.dtype),) * 2,
        in_specs=[anywhere] * 2,
        out_specs=(anywhere,) * 2,
        scratch_shapes=[
            pltpu.SemaphoreType.DMA((2, count)),
            pltpu.SemaphoreType.DMA((2, count)),
            pltpu.SemaphoreType.DMA((2,)),
        ],
        compiler_params=pltpu.CompilerParams(collective_id=0, has_side_effects=True),
    )(tokens, cotangent)


def parts_kernel(group, block_ref, live_ref, tok_ref, cot_ref, *refs):
    gates, ups, downs = refs[:group], refs[group : 2 * group], refs[2 * group : 3 * group]
    out_ref = refs[3 * group]
    row, step = pl.program_id(0), pl.program_id(1)
    tok, cot = tok_ref[...], cot_ref[...]
    owners, _, own_rows, _ = out_ref.shape
    for at in range(group):
        live = live_ref[row, step * group + at] == 1
        columns = slice(at * BLK, (at + 1) * BLK)
        gate = jnp.dot(tok, gates[at][...], preferred_element_type=jnp.float32)
        up = jnp.dot(tok, ups[at][...], preferred_element_type=jnp.float32)
        grad = lax.dot_general(
            cot, downs[at][...], (((1,), (1,)), ((), ())), preferred_element_type=jnp.float32
        )
        up = jnp.where(live, up, 0.0)
        grad = jnp.where(live, grad, 0.0)
        for which, value in enumerate((gate, up, grad)):
            out_ref[:, which, :, columns] = value.reshape(owners, own_rows, BLK)


def weight_specs(group, feats):
    def columns(at):
        return pl.BlockSpec(
            (feats, BLK), lambda row, step, block, live: (0, block[row, step * group + at])
        )

    def rows(at):
        return pl.BlockSpec(
            (BLK, feats), lambda row, step, block, live: (block[row, step * group + at], 0)
        )

    return (
        [columns(at) for at in range(group)] * 2 + [rows(at) for at in range(group)]
    )


def partial_products(block, live, tok, cot, gate_w, up_w, down_w, own_rows):
    row_blocks, capacity = block.shape
    feats = tok.shape[1]
    group = group_of(capacity)
    owners = ROWBLK // own_rows
    rows_spec = pl.BlockSpec((ROWBLK, feats), lambda row, step, block, live: (row, 0))
    flops = 6 * row_blocks * ROWBLK * feats * capacity * BLK
    return pl.pallas_call(
        functools.partial(parts_kernel, group),
        out_shape=jax.ShapeDtypeStruct(
            (row_blocks * owners, 3, own_rows, capacity * BLK), jnp.float32
        ),
        grid_spec=pltpu.PrefetchScalarGridSpec(
            num_scalar_prefetch=2,
            grid=(row_blocks, capacity // group),
            in_specs=[rows_spec, rows_spec] + weight_specs(group, feats),
            out_specs=pl.BlockSpec(
                (owners, 3, own_rows, group * BLK), lambda row, step, block, live: (row, 0, 0, step)
            ),
        ),
        compiler_params=pltpu.CompilerParams(vmem_limit_bytes=VMEM_LIMIT),
        cost_estimate=pl.CostEstimate(
            flops=flops, bytes_accessed=flops // ROWBLK, transcendentals=0
        ),
    )(block, live, tok, cot, *([gate_w] * group + [up_w] * group + [down_w] * group))


def exchange_kernel(
    count, part_ref, all_ref, paired, summed, landed, acts,
    pair_send, pair_recv, sum_send, sum_recv, all_send, all_recv, hand_send, hand_recv, own_sem,
):
    chips = count // 2
    me = lax.axis_index("seq")
    chip, core = me // 2, lax.rem(me, 2)
    sibling = me + 1 - 2 * core
    columns = part_ref.shape[3]
    piece = group_of(columns // BLK) * BLK

    def ahead(shift):
        return lax.rem(chip + shift, chips)

    def behind(shift):
        return lax.rem(chip + chips - shift, chips)

    barrier = pltpu.get_barrier_semaphore()
    pl.semaphore_signal(barrier, inc=1, device_id={"seq": sibling}, device_id_type=MESH)
    for shift in range(1, chips):
        pl.semaphore_signal(
            barrier, inc=1, device_id={"seq": ahead(shift) * 2 + core}, device_id_type=MESH
        )
    pl.semaphore_wait(barrier, chips)

    def pair_copy(shift):
        return pltpu.make_async_remote_copy(
            src_ref=part_ref.at[ahead(shift) * 2 + 1 - core],
            dst_ref=paired.at[shift],
            send_sem=pair_send.at[shift],
            recv_sem=pair_recv.at[shift],
            device_id={"seq": sibling},
            device_id_type=MESH,
        )

    def sum_copy(shift):
        return pltpu.make_async_remote_copy(
            src_ref=summed.at[shift],
            dst_ref=landed.at[shift],
            send_sem=sum_send.at[shift],
            recv_sem=sum_recv.at[shift],
            device_id={"seq": ahead(shift) * 2 + core},
            device_id_type=MESH,
        )

    def all_copy(shift, owner):
        return pltpu.make_async_remote_copy(
            src_ref=acts,
            dst_ref=all_ref.at[owner],
            send_sem=all_send.at[shift],
            recv_sem=all_recv.at[shift],
            device_id={"seq": ahead(shift) * 2 + core},
            device_id_type=MESH,
        )

    def hand_copy(shift, owner):
        return pltpu.make_async_remote_copy(
            src_ref=all_ref.at[owner],
            dst_ref=all_ref.at[owner],
            send_sem=hand_send.at[shift],
            recv_sem=hand_recv.at[shift],
            device_id={"seq": sibling},
            device_id_type=MESH,
        )

    for shift in list(range(1, chips)) + [0]:
        pair_copy(shift).start()

    def send_sum(shift, carry):
        pair_copy(shift).wait_recv()
        mine = ahead(shift) * 2 + core
        for which in range(3):
            for start in range(0, columns, piece):
                cut = slice(start, start + piece)
                summed[shift, which, :, cut] = (
                    part_ref[mine, which, :, cut] + paired[shift, which, :, cut]
                ).astype(jnp.bfloat16)
        sum_copy(shift).start()
        return carry

    lax.fori_loop(1, chips, send_sum, 0)
    pair_copy(0).wait_recv()

    def arrived(shift, carry):
        sum_copy(shift).wait_recv()
        return carry

    lax.fori_loop(1, chips, arrived, 0)

    def act(step, carry):
        cut = pl.ds(pl.multiple_of(step * piece, BLK), piece)

        def total(which):
            value = part_ref[me, which, :, cut] + paired[0, which, :, cut]
            for shift in range(1, chips):
                value = value + landed[shift, which, :, cut].astype(jnp.float32)
            return value

        gate, up, grad = total(0), total(1), total(2)
        sig = jax.nn.sigmoid(gate)
        acts[0, :, cut] = (gate * sig * up).astype(jnp.bfloat16)
        acts[1, :, cut] = (grad * up * sig * (1.0 + gate * (1.0 - sig))).astype(jnp.bfloat16)
        acts[2, :, cut] = (grad * gate * sig).astype(jnp.bfloat16)
        return carry

    lax.fori_loop(0, columns // piece, act, 0)

    for shift in range(1, chips):
        all_copy(shift, me).start()
    own = pltpu.make_async_copy(acts, all_ref.at[me], own_sem)
    own.start()
    first = pltpu.make_async_remote_copy(
        src_ref=acts,
        dst_ref=all_ref.at[me],
        send_sem=hand_send.at[0],
        recv_sem=hand_recv.at[0],
        device_id={"seq": sibling},
        device_id_type=MESH,
    )
    first.start()

    def hand(shift, carry):
        owner = behind(shift) * 2 + core
        all_copy(shift, owner).wait_recv()
        hand_copy(shift, owner).start()
        return carry

    lax.fori_loop(1, chips, hand, 0)
    own.wait()
    first.wait_send()

    def finish(shift, carry):
        hand_copy(shift, behind(shift) * 2 + 1 - core).wait_recv()
        pair_copy(shift).wait_send()
        return carry

    lax.fori_loop(0, chips, finish, 0)

    def sent(shift, carry):
        sum_copy(shift).wait_send()
        all_copy(shift, me).wait_send()
        hand_copy(shift, behind(shift) * 2 + core).wait_send()
        return carry

    lax.fori_loop(1, chips, sent, 0)


def exchange(parts):
    count = lax.axis_size("seq")
    chips = count // 2
    chunk = parts.shape[1:]
    sems = [pltpu.SemaphoreType.DMA((chips,))] * 8
    return pl.pallas_call(
        functools.partial(exchange_kernel, count),
        out_shape=jax.ShapeDtypeStruct(parts.shape, jnp.bfloat16),
        in_specs=[pl.BlockSpec(memory_space=pltpu.VMEM)],
        out_specs=pl.BlockSpec(memory_space=pl.ANY),
        scratch_shapes=[
            pltpu.VMEM((chips,) + chunk, jnp.float32),
            pltpu.VMEM((chips,) + chunk, jnp.bfloat16),
            pltpu.VMEM((chips,) + chunk, jnp.bfloat16),
            pltpu.VMEM(chunk, jnp.bfloat16),
        ]
        + sems
        + [pltpu.SemaphoreType.DMA],
        compiler_params=pltpu.CompilerParams(
            collective_id=1, has_side_effects=True, vmem_limit_bytes=VMEM_LIMIT
        ),
    )(parts)


def rows_out_kernel(group, block_ref, live_ref, act_ref, *refs):
    gates, ups, downs = refs[:group], refs[group : 2 * group], refs[2 * group : 3 * group]
    out_ref = refs[3 * group]
    step = pl.program_id(1)

    @pl.when(step == 0)
    def _():
        out_ref[...] = jnp.zeros_like(out_ref)

    out = jnp.zeros(out_ref.shape[2:], jnp.float32)
    grad = jnp.zeros(out_ref.shape[2:], jnp.float32)
    across = (((1,), (1,)), ((), ()))
    for at in range(group):
        columns = slice(at * BLK, (at + 1) * BLK)
        hid, dgate, dup = (act_ref[:, which, :, columns].reshape(ROWBLK, BLK) for which in range(3))
        out += jnp.dot(hid, downs[at][...], preferred_element_type=jnp.float32)
        grad += lax.dot_general(dgate, gates[at][...], across, preferred_element_type=jnp.float32)
        grad += lax.dot_general(dup, ups[at][...], across, preferred_element_type=jnp.float32)
    out_ref[0, 0] += out
    out_ref[0, 1] += grad


def rows_out(block, live, acts, gate_w, up_w, down_w):
    row_blocks, capacity = block.shape
    own_rows = acts.shape[2]
    feats = gate_w.shape[0]
    group = group_of(capacity)
    owners = ROWBLK // own_rows
    flops = 6 * row_blocks * ROWBLK * feats * capacity * BLK
    return pl.pallas_call(
        functools.partial(rows_out_kernel, group),
        out_shape=jax.ShapeDtypeStruct((row_blocks, 2, ROWBLK, feats), jnp.float32),
        grid_spec=pltpu.PrefetchScalarGridSpec(
            num_scalar_prefetch=2,
            grid=(row_blocks, capacity // group),
            in_specs=[
                pl.BlockSpec(
                    (owners, 3, own_rows, group * BLK),
                    lambda row, step, block, live: (row, 0, 0, step),
                )
            ]
            + weight_specs(group, feats),
            out_specs=pl.BlockSpec(
                (1, 2, ROWBLK, feats), lambda row, step, block, live: (row, 0, 0, 0)
            ),
        ),
        compiler_params=pltpu.CompilerParams(vmem_limit_bytes=VMEM_LIMIT),
        cost_estimate=pl.CostEstimate(
            flops=flops, bytes_accessed=flops // ROWBLK, transcendentals=0
        ),
    )(block, live, acts, *([gate_w] * group + [up_w] * group + [down_w] * group))


def weights_out_kernel(
    group, scale, slot_ref, mask_ref, tok_ref, cot_ref, act_ref, gate_ref, up_ref, down_ref,
    flipped, dense,
):
    step = pl.program_id(0)
    row_blocks = mask_ref.shape[0]
    owners = ROWBLK // act_ref.shape[2]

    @pl.when(step == 0)
    def _():
        flipped[...] = tok_ref[...].T

    for at in range(group):
        for row in range(row_blocks):
            kept = mask_ref[row, step * group + at] == 1
            slot = pl.ds(pl.multiple_of(slot_ref[row, step * group + at] * BLK, BLK), BLK)
            for which in range(3):
                value = act_ref[row * owners : (row + 1) * owners, which, :, slot]
                value = jnp.where(kept, value, jnp.zeros_like(value))
                dense[which, row * ROWBLK : (row + 1) * ROWBLK, at * BLK : (at + 1) * BLK] = (
                    value.reshape(ROWBLK, BLK)
                )
    tok = flipped[...]
    gate_ref[...] = jnp.dot(tok, dense[1], preferred_element_type=jnp.float32) * scale
    up_ref[...] = jnp.dot(tok, dense[2], preferred_element_type=jnp.float32) * scale
    down_ref[...] = (
        lax.dot_general(
            dense[0], cot_ref[...], (((0,), (0,)), ((), ())), preferred_element_type=jnp.float32
        )
        * scale
    )


def weights_out(slots, masks, tok, cot, acts):
    row_blocks, blocks = masks.shape
    rows, feats = tok.shape
    group = group_of(blocks)
    whole = pl.BlockSpec((rows, feats), lambda step, slot, mask: (0, 0))
    wide = pl.BlockSpec((feats, group * BLK), lambda step, slot, mask: (0, step))
    hidden = blocks * BLK
    return pl.pallas_call(
        functools.partial(weights_out_kernel, group, 1.0 / math.sqrt(rows)),
        out_shape=(
            jax.ShapeDtypeStruct((feats, hidden), jnp.float32),
            jax.ShapeDtypeStruct((feats, hidden), jnp.float32),
            jax.ShapeDtypeStruct((hidden, feats), jnp.float32),
        ),
        grid_spec=pltpu.PrefetchScalarGridSpec(
            num_scalar_prefetch=2,
            grid=(blocks // group,),
            in_specs=[
                whole,
                whole,
                pl.BlockSpec(acts.shape, lambda step, slot, mask: (0, 0, 0, 0)),
            ],
            out_specs=(
                wide,
                wide,
                pl.BlockSpec((group * BLK, feats), lambda step, slot, mask: (step, 0)),
            ),
            scratch_shapes=[
                pltpu.VMEM((feats, rows), jnp.bfloat16),
                pltpu.VMEM((3, rows, group * BLK), jnp.bfloat16),
            ],
        ),
        compiler_params=pltpu.CompilerParams(vmem_limit_bytes=VMEM_LIMIT),
        cost_estimate=pl.CostEstimate(
            flops=6 * rows * feats * hidden, bytes_accessed=12 * feats * hidden, transcendentals=0
        ),
    )(slots, masks, tok, cot, acts)


def shards(tokens, gate_weight, up_weight, down_weight, masks, cotangent):
    seq_count = lax.axis_size("seq")
    tp_count = lax.axis_size("tp")
    rank = lax.axis_index("tp")
    rows, feats = tokens.shape
    total_rows = rows * tp_count
    kept_total = masks.shape[1] * tp_count // KEEP_PART
    capacity = min(2 * kept_total // tp_count, masks.shape[1])
    tok, cot = (value.reshape(total_rows, feats) for value in gather_rows(tokens, cotangent))
    block, live, slots = slot_tables(masks, capacity)
    parts = partial_products(
        block, live, tok, cot, gate_weight, up_weight, down_weight, total_rows // seq_count
    )
    acts = exchange(parts)
    row_parts = rows_out(block, live, acts, gate_weight, up_weight, down_weight)
    row_parts = jnp.swapaxes(row_parts.reshape(tp_count, rows // ROWBLK, 2, ROWBLK, feats), 1, 2)
    moved = []
    for shift in range(1, tp_count):
        piece = lax.dynamic_index_in_dim(
            row_parts, lax.rem(rank + shift, tp_count), 0, keepdims=False
        ).astype(jnp.bfloat16)
        pairs = [(src, (src + shift) % tp_count) for src in range(tp_count)]
        moved.append(lax.ppermute(piece, "tp", pairs))
    grad_gate, grad_up, grad_down = weights_out(slots, masks, tok, cot, acts)
    mine = lax.dynamic_index_in_dim(row_parts, rank, 0, keepdims=False)
    for piece in moved:
        mine = mine + piece.astype(jnp.float32)
    mine = mine.reshape(2, rows, feats).astype(jnp.bfloat16)
    return (mine[0], mine[1], grad_gate, grad_up, grad_down)


def solution(mesh):
    placed = (
        P("tp", "seq"),
        P("seq", "tp"),
        P("seq", "tp"),
        P("tp", "seq"),
        P(None, "tp"),
        P("tp", "seq"),
    )
    return jax.shard_map(
        shards,
        mesh=mesh,
        in_specs=placed,
        out_specs=(P("tp", "seq"), P("tp", "seq"), P("seq", "tp"), P("seq", "tp"), P("tp", "seq")),
        check_vma=False,
    )
```

```python
import functools
import math

import jax
import jax.numpy as jnp
from jax import lax
from jax.experimental import pallas as pl
from jax.experimental.pallas import tpu as pltpu
from jax.sharding import PartitionSpec as P

BLK = 128
ROWBLK = 128
KEEP_PART = 4
MESH = pl.DeviceIdType.MESH
VMEM_LIMIT = 60 * 1024 * 1024


def group_of(count):
    for size in (7, 8, 4, 2):
        if count % size == 0:
            return size
    return 1


def tables_kernel(mask_ref, block_ref, live_ref, slot_ref):
    row_blocks, blocks = mask_ref.shape
    capacity = block_ref.shape[1]
    for row in range(row_blocks):
        for slot in range(capacity):
            block_ref[row, slot] = 0
            live_ref[row, slot] = 0

        def step(block, taken, row=row):
            kept = mask_ref[row, block]
            at = jnp.minimum(taken, capacity - 1)
            slot_ref[row, block] = at

            @pl.when(kept == 1)
            def _():
                block_ref[row, at] = block
                live_ref[row, at] = 1

            return taken + kept

        lax.fori_loop(0, blocks, step, jnp.int32(0))


def slot_tables(masks, capacity):
    row_blocks, blocks = masks.shape
    smem = pl.BlockSpec(memory_space=pltpu.SMEM)
    return pl.pallas_call(
        tables_kernel,
        out_shape=(
            jax.ShapeDtypeStruct((row_blocks, capacity), jnp.int32),
            jax.ShapeDtypeStruct((row_blocks, capacity), jnp.int32),
            jax.ShapeDtypeStruct((row_blocks, blocks), jnp.int32),
        ),
        in_specs=[smem],
        out_specs=(smem, smem, smem),
    )(masks)


def rows_kernel(count, tok_ref, cot_ref, tok_all, cot_all, send_sem, recv_sem, own_sem):
    me = lax.axis_index("tp")
    barrier = pltpu.get_barrier_semaphore()
    for shift in range(1, count):
        pl.semaphore_signal(
            barrier, inc=1, device_id={"tp": lax.rem(me + shift, count)}, device_id_type=MESH
        )
    pl.semaphore_wait(barrier, count - 1)
    copies = []
    for which, (src, dst) in enumerate(((tok_ref, tok_all), (cot_ref, cot_all))):
        for shift in range(1, count):
            copy = pltpu.make_async_remote_copy(
                src_ref=src,
                dst_ref=dst.at[me],
                send_sem=send_sem.at[which, shift],
                recv_sem=recv_sem.at[which, shift],
                device_id={"tp": lax.rem(me + shift, count)},
                device_id_type=MESH,
            )
            copy.start()
            copies.append(copy)
        own = pltpu.make_async_copy(src, dst.at[me], own_sem.at[which])
        own.start()
        copies.append(own)
    for copy in copies:
        copy.wait()


def gather_rows(tokens, cotangent):
    count = lax.axis_size("tp")
    rows, feats = tokens.shape
    anywhere = pl.BlockSpec(memory_space=pl.ANY)
    return pl.pallas_call(
        functools.partial(rows_kernel, count),
        out_shape=(jax.ShapeDtypeStruct((count, rows, feats), tokens.dtype),) * 2,
        in_specs=[anywhere] * 2,
        out_specs=(anywhere,) * 2,
        scratch_shapes=[
            pltpu.SemaphoreType.DMA((2, count)),
            pltpu.SemaphoreType.DMA((2, count)),
            pltpu.SemaphoreType.DMA((2,)),
        ],
        compiler_params=pltpu.CompilerParams(collective_id=0, has_side_effects=True),
    )(tokens, cotangent)


def parts_kernel(group, block_ref, live_ref, tok_ref, cot_ref, *refs):
    gates, ups, downs = refs[:group], refs[group : 2 * group], refs[2 * group : 3 * group]
    out_ref = refs[3 * group]
    row, step = pl.program_id(0), pl.program_id(1)
    tok, cot = tok_ref[...], cot_ref[...]
    owners, _, own_rows, _ = out_ref.shape
    for at in range(group):
        live = live_ref[row, step * group + at] == 1
        columns = slice(at * BLK, (at + 1) * BLK)
        gate = jnp.dot(tok, gates[at][...], preferred_element_type=jnp.float32)
        up = jnp.dot(tok, ups[at][...], preferred_element_type=jnp.float32)
        grad = lax.dot_general(
            cot, downs[at][...], (((1,), (1,)), ((), ())), preferred_element_type=jnp.float32
        )
        up = jnp.where(live, up, 0.0)
        grad = jnp.where(live, grad, 0.0)
        for which, value in enumerate((gate, up, grad)):
            out_ref[:, which, :, columns] = value.reshape(owners, own_rows, BLK)


def weight_specs(group, feats):
    def columns(at):
        return pl.BlockSpec(
            (feats, BLK), lambda row, step, block, live: (0, block[row, step * group + at])
        )

    def rows(at):
        return pl.BlockSpec(
            (BLK, feats), lambda row, step, block, live: (block[row, step * group + at], 0)
        )

    return (
        [columns(at) for at in range(group)] * 2 + [rows(at) for at in range(group)]
    )


def partial_products(block, live, tok, cot, gate_w, up_w, down_w, own_rows):
    row_blocks, capacity = block.shape
    feats = tok.shape[1]
    group = group_of(capacity)
    owners = ROWBLK // own_rows
    rows_spec = pl.BlockSpec((ROWBLK, feats), lambda row, step, block, live: (row, 0))
    flops = 6 * row_blocks * ROWBLK * feats * capacity * BLK
    return pl.pallas_call(
        functools.partial(parts_kernel, group),
        out_shape=jax.ShapeDtypeStruct(
            (row_blocks * owners, 3, own_rows, capacity * BLK), jnp.float32
        ),
        grid_spec=pltpu.PrefetchScalarGridSpec(
            num_scalar_prefetch=2,
            grid=(row_blocks, capacity // group),
            in_specs=[rows_spec, rows_spec] + weight_specs(group, feats),
            out_specs=pl.BlockSpec(
                (owners, 3, own_rows, group * BLK), lambda row, step, block, live: (row, 0, 0, step)
            ),
        ),
        compiler_params=pltpu.CompilerParams(vmem_limit_bytes=VMEM_LIMIT),
        cost_estimate=pl.CostEstimate(
            flops=flops, bytes_accessed=flops // ROWBLK, transcendentals=0
        ),
    )(block, live, tok, cot, *([gate_w] * group + [up_w] * group + [down_w] * group))


def exchange_kernel(
    count, part_ref, all_ref, paired, summed, landed, acts,
    pair_send, pair_recv, sum_send, sum_recv, side_send, up_send, down_send, all_recv,
    hand_send, hand_recv, own_sem,
):
    chips = count // 2
    me = lax.axis_index("seq")
    chip, core = me // 2, lax.rem(me, 2)
    sibling = me + 1 - 2 * core
    tall = 4 if chips % 4 == 0 else chips
    wide = chips // tall
    along, across = chip // wide, lax.rem(chip, wide)
    columns = part_ref.shape[3]
    piece = group_of(columns // BLK) * BLK

    def ahead(shift):
        return lax.rem(chip + shift, chips)

    barrier = pltpu.get_barrier_semaphore()
    pl.semaphore_signal(barrier, inc=1, device_id={"seq": sibling}, device_id_type=MESH)
    for shift in range(1, chips):
        pl.semaphore_signal(
            barrier, inc=1, device_id={"seq": ahead(shift) * 2 + core}, device_id_type=MESH
        )
    pl.semaphore_wait(barrier, chips)

    def pair_copy(shift):
        return pltpu.make_async_remote_copy(
            src_ref=part_ref.at[ahead(shift) * 2 + 1 - core],
            dst_ref=paired.at[shift],
            send_sem=pair_send.at[shift],
            recv_sem=pair_recv.at[shift],
            device_id={"seq": sibling},
            device_id_type=MESH,
        )

    def sum_copy(shift):
        return pltpu.make_async_remote_copy(
            src_ref=summed.at[shift],
            dst_ref=landed.at[shift],
            send_sem=sum_send.at[shift],
            recv_sem=sum_recv.at[shift],
            device_id={"seq": ahead(shift) * 2 + core},
            device_id_type=MESH,
        )

    def route(owner, dest, send, src=None):
        slot = all_ref.at[owner * 2 + core]
        return pltpu.make_async_remote_copy(
            src_ref=slot if src is None else src,
            dst_ref=slot,
            send_sem=send.at[owner],
            recv_sem=all_recv.at[owner],
            device_id={"seq": dest * 2 + core},
            device_id_type=MESH,
        )

    def hand_copy(owner, side, src=None):
        slot = all_ref.at[owner * 2 + side]
        return pltpu.make_async_remote_copy(
            src_ref=slot if src is None else src,
            dst_ref=slot,
            send_sem=hand_send.at[owner],
            recv_sem=hand_recv.at[owner],
            device_id={"seq": sibling},
            device_id_type=MESH,
        )

    for shift in list(range(1, chips)) + [0]:
        pair_copy(shift).start()

    def send_sum(shift, carry):
        pair_copy(shift).wait_recv()
        mine = ahead(shift) * 2 + core
        for which in range(3):
            for start in range(0, columns, piece):
                cut = slice(start, start + piece)
                summed[shift, which, :, cut] = (
                    part_ref[mine, which, :, cut] + paired[shift, which, :, cut]
                ).astype(jnp.bfloat16)
        sum_copy(shift).start()
        return carry

    lax.fori_loop(1, chips, send_sum, 0)
    pair_copy(0).wait_recv()

    def arrived(shift, carry):
        sum_copy(shift).wait_recv()
        return carry

    lax.fori_loop(1, chips, arrived, 0)

    def act(step, carry):
        cut = pl.ds(pl.multiple_of(step * piece, BLK), piece)

        def total(which):
            value = part_ref[me, which, :, cut] + paired[0, which, :, cut]
            for shift in range(1, chips):
                value = value + landed[shift, which, :, cut].astype(jnp.float32)
            return value

        gate, up, grad = total(0), total(1), total(2)
        sig = jax.nn.sigmoid(gate)
        acts[0, :, cut] = (gate * sig * up).astype(jnp.bfloat16)
        acts[1, :, cut] = (grad * up * sig * (1.0 + gate * (1.0 - sig))).astype(jnp.bfloat16)
        acts[2, :, cut] = (grad * gate * sig).astype(jnp.bfloat16)
        return carry

    lax.fori_loop(0, columns // piece, act, 0)

    own = pltpu.make_async_copy(acts, all_ref.at[me], own_sem)
    own.start()

    def aside(step):
        return lax.rem(across + step, wide)

    def pass_on(owner, up, down, src=None):
        @pl.when(jnp.logical_and(up, along < tall - 1))
        def _():
            route(owner, chip + wide, up_send, src).start()

        @pl.when(jnp.logical_and(down, along > 0))
        def _():
            route(owner, chip - wide, down_send, src).start()

        hand_copy(owner, core, src).start()

    def take(owner):
        route(owner, chip, up_send).wait_recv()

    yes, no = jnp.bool_(True), jnp.bool_(False)
    for step in range(1, wide):
        pltpu.make_async_remote_copy(
            src_ref=acts,
            dst_ref=all_ref.at[me],
            send_sem=side_send.at[step],
            recv_sem=all_recv.at[chip],
            device_id={"seq": (along * wide + aside(step)) * 2 + core},
            device_id_type=MESH,
        ).start()
    pass_on(chip, yes, yes, acts)
    for step in range(1, wide):
        owner = along * wide + aside(step)
        take(owner)
        pass_on(owner, yes, yes)
    for far in range(1, tall):
        for step in range(wide):

            @pl.when(along >= far)
            def _():
                owner = (along - far) * wide + aside(step)
                take(owner)
                pass_on(owner, yes, no)

            @pl.when(along + far < tall)
            def _():
                owner = (along + far) * wide + aside(step)
                take(owner)
                pass_on(owner, no, yes)

    own.wait()
    for step in range(1, wide):
        pltpu.make_async_remote_copy(
            src_ref=acts,
            dst_ref=all_ref.at[me],
            send_sem=side_send.at[step],
            recv_sem=all_recv.at[chip],
            device_id={"seq": (along * wide + aside(step)) * 2 + core},
            device_id_type=MESH,
        ).wait_send()

    def finish(owner, carry):
        hand_copy(owner, 1 - core).wait_recv()
        hand_copy(owner, core).wait_send()
        pair_copy(owner).wait_send()

        @pl.when(jnp.logical_and(owner // wide <= along, along < tall - 1))
        def _():
            route(owner, chip + wide, up_send).wait_send()

        @pl.when(jnp.logical_and(owner // wide >= along, along > 0))
        def _():
            route(owner, chip - wide, down_send).wait_send()

        return carry

    lax.fori_loop(0, chips, finish, 0)

    def sent(shift, carry):
        sum_copy(shift).wait_send()
        return carry

    lax.fori_loop(1, chips, sent, 0)


def exchange(parts):
    count = lax.axis_size("seq")
    chips = count // 2
    chunk = parts.shape[1:]
    sems = [pltpu.SemaphoreType.DMA((chips,))] * 10
    return pl.pallas_call(
        functools.partial(exchange_kernel, count),
        out_shape=jax.ShapeDtypeStruct(parts.shape, jnp.bfloat16),
        in_specs=[pl.BlockSpec(memory_space=pltpu.VMEM)],
        out_specs=pl.BlockSpec(memory_space=pl.ANY),
        scratch_shapes=[
            pltpu.VMEM((chips,) + chunk, jnp.float32),
            pltpu.VMEM((chips,) + chunk, jnp.bfloat16),
            pltpu.VMEM((chips,) + chunk, jnp.bfloat16),
            pltpu.VMEM(chunk, jnp.bfloat16),
        ]
        + sems
        + [pltpu.SemaphoreType.DMA],
        compiler_params=pltpu.CompilerParams(
            collective_id=1, has_side_effects=True, vmem_limit_bytes=VMEM_LIMIT
        ),
    )(parts)


def rows_out_kernel(group, block_ref, live_ref, act_ref, *refs):
    gates, ups, downs = refs[:group], refs[group : 2 * group], refs[2 * group : 3 * group]
    out_ref = refs[3 * group]
    step = pl.program_id(1)

    @pl.when(step == 0)
    def _():
        out_ref[...] = jnp.zeros_like(out_ref)

    out = jnp.zeros(out_ref.shape[2:], jnp.float32)
    grad = jnp.zeros(out_ref.shape[2:], jnp.float32)
    across = (((1,), (1,)), ((), ()))
    for at in range(group):
        columns = slice(at * BLK, (at + 1) * BLK)
        hid, dgate, dup = (act_ref[:, which, :, columns].reshape(ROWBLK, BLK) for which in range(3))
        out += jnp.dot(hid, downs[at][...], preferred_element_type=jnp.float32)
        grad += lax.dot_general(dgate, gates[at][...], across, preferred_element_type=jnp.float32)
        grad += lax.dot_general(dup, ups[at][...], across, preferred_element_type=jnp.float32)
    out_ref[0, 0] += out
    out_ref[0, 1] += grad


def rows_out(block, live, acts, gate_w, up_w, down_w):
    row_blocks, capacity = block.shape
    own_rows = acts.shape[2]
    feats = gate_w.shape[0]
    group = group_of(capacity)
    owners = ROWBLK // own_rows
    flops = 6 * row_blocks * ROWBLK * feats * capacity * BLK
    return pl.pallas_call(
        functools.partial(rows_out_kernel, group),
        out_shape=jax.ShapeDtypeStruct((row_blocks, 2, ROWBLK, feats), jnp.float32),
        grid_spec=pltpu.PrefetchScalarGridSpec(
            num_scalar_prefetch=2,
            grid=(row_blocks, capacity // group),
            in_specs=[
                pl.BlockSpec(
                    (owners, 3, own_rows, group * BLK),
                    lambda row, step, block, live: (row, 0, 0, step),
                )
            ]
            + weight_specs(group, feats),
            out_specs=pl.BlockSpec(
                (1, 2, ROWBLK, feats), lambda row, step, block, live: (row, 0, 0, 0)
            ),
        ),
        compiler_params=pltpu.CompilerParams(vmem_limit_bytes=VMEM_LIMIT),
        cost_estimate=pl.CostEstimate(
            flops=flops, bytes_accessed=flops // ROWBLK, transcendentals=0
        ),
    )(block, live, acts, *([gate_w] * group + [up_w] * group + [down_w] * group))


def weights_out_kernel(
    group, scale, slot_ref, mask_ref, tok_ref, cot_ref, act_ref, gate_ref, up_ref, down_ref,
    flipped, dense,
):
    step = pl.program_id(0)
    row_blocks = mask_ref.shape[0]
    owners = ROWBLK // act_ref.shape[2]

    @pl.when(step == 0)
    def _():
        flipped[...] = tok_ref[...].T

    for at in range(group):
        for row in range(row_blocks):
            kept = mask_ref[row, step * group + at] == 1
            slot = pl.ds(pl.multiple_of(slot_ref[row, step * group + at] * BLK, BLK), BLK)
            for which in range(3):
                value = act_ref[row * owners : (row + 1) * owners, which, :, slot]
                value = jnp.where(kept, value, jnp.zeros_like(value))
                dense[which, row * ROWBLK : (row + 1) * ROWBLK, at * BLK : (at + 1) * BLK] = (
                    value.reshape(ROWBLK, BLK)
                )
    tok = flipped[...]
    gate_ref[...] = jnp.dot(tok, dense[1], preferred_element_type=jnp.float32) * scale
    up_ref[...] = jnp.dot(tok, dense[2], preferred_element_type=jnp.float32) * scale
    down_ref[...] = (
        lax.dot_general(
            dense[0], cot_ref[...], (((0,), (0,)), ((), ())), preferred_element_type=jnp.float32
        )
        * scale
    )


def weights_out(slots, masks, tok, cot, acts):
    row_blocks, blocks = masks.shape
    rows, feats = tok.shape
    group = group_of(blocks)
    whole = pl.BlockSpec((rows, feats), lambda step, slot, mask: (0, 0))
    wide = pl.BlockSpec((feats, group * BLK), lambda step, slot, mask: (0, step))
    hidden = blocks * BLK
    return pl.pallas_call(
        functools.partial(weights_out_kernel, group, 1.0 / math.sqrt(rows)),
        out_shape=(
            jax.ShapeDtypeStruct((feats, hidden), jnp.float32),
            jax.ShapeDtypeStruct((feats, hidden), jnp.float32),
            jax.ShapeDtypeStruct((hidden, feats), jnp.float32),
        ),
        grid_spec=pltpu.PrefetchScalarGridSpec(
            num_scalar_prefetch=2,
            grid=(blocks // group,),
            in_specs=[
                whole,
                whole,
                pl.BlockSpec(acts.shape, lambda step, slot, mask: (0, 0, 0, 0)),
            ],
            out_specs=(
                wide,
                wide,
                pl.BlockSpec((group * BLK, feats), lambda step, slot, mask: (step, 0)),
            ),
            scratch_shapes=[
                pltpu.VMEM((feats, rows), jnp.bfloat16),
                pltpu.VMEM((3, rows, group * BLK), jnp.bfloat16),
            ],
        ),
        compiler_params=pltpu.CompilerParams(vmem_limit_bytes=VMEM_LIMIT),
        cost_estimate=pl.CostEstimate(
            flops=6 * rows * feats * hidden, bytes_accessed=12 * feats * hidden, transcendentals=0
        ),
    )(slots, masks, tok, cot, acts)


def shards(tokens, gate_weight, up_weight, down_weight, masks, cotangent):
    seq_count = lax.axis_size("seq")
    tp_count = lax.axis_size("tp")
    rank = lax.axis_index("tp")
    rows, feats = tokens.shape
    total_rows = rows * tp_count
    kept_total = masks.shape[1] * tp_count // KEEP_PART
    capacity = min(2 * kept_total // tp_count, masks.shape[1])
    tok, cot = (value.reshape(total_rows, feats) for value in gather_rows(tokens, cotangent))
    block, live, slots = slot_tables(masks, capacity)
    parts = partial_products(
        block, live, tok, cot, gate_weight, up_weight, down_weight, total_rows // seq_count
    )
    acts = exchange(parts)
    row_parts = rows_out(block, live, acts, gate_weight, up_weight, down_weight)
    row_parts = jnp.swapaxes(row_parts.reshape(tp_count, rows // ROWBLK, 2, ROWBLK, feats), 1, 2)
    moved = []
    for shift in range(1, tp_count):
        piece = lax.dynamic_index_in_dim(
            row_parts, lax.rem(rank + shift, tp_count), 0, keepdims=False
        ).astype(jnp.bfloat16)
        pairs = [(src, (src + shift) % tp_count) for src in range(tp_count)]
        moved.append(lax.ppermute(piece, "tp", pairs))
    grad_gate, grad_up, grad_down = weights_out(slots, masks, tok, cot, acts)
    mine = lax.dynamic_index_in_dim(row_parts, rank, 0, keepdims=False)
    for piece in moved:
        mine = mine + piece.astype(jnp.float32)
    mine = mine.reshape(2, rows, feats).astype(jnp.bfloat16)
    return (mine[0], mine[1], grad_gate, grad_up, grad_down)


def solution(mesh):
    placed = (
        P("tp", "seq"),
        P("seq", "tp"),
        P("seq", "tp"),
        P("tp", "seq"),
        P(None, "tp"),
        P("tp", "seq"),
    )
    return jax.shard_map(
        shards,
        mesh=mesh,
        in_specs=placed,
        out_specs=(P("tp", "seq"), P("tp", "seq"), P("seq", "tp"), P("seq", "tp"), P("tp", "seq")),
        check_vma=False,
    )
```

```python
import functools
import math

import jax
import jax.numpy as jnp
from jax import lax
from jax.experimental import pallas as pl
from jax.experimental.pallas import tpu as pltpu
from jax.sharding import PartitionSpec as P

BLK = 128
ROWBLK = 128
KEEP_PART = 4
MESH = pl.DeviceIdType.MESH
VMEM_LIMIT = 60 * 1024 * 1024


def group_of(count):
    for size in (7, 8, 4, 2):
        if count % size == 0:
            return size
    return 1


def tables_kernel(mask_ref, block_ref, live_ref, slot_ref):
    row_blocks, blocks = mask_ref.shape
    capacity = block_ref.shape[1]
    for row in range(row_blocks):
        for slot in range(capacity):
            block_ref[row, slot] = 0
            live_ref[row, slot] = 0

        def step(block, taken, row=row):
            kept = mask_ref[row, block]
            at = jnp.minimum(taken, capacity - 1)
            slot_ref[row, block] = at

            @pl.when(kept == 1)
            def _():
                block_ref[row, at] = block
                live_ref[row, at] = 1

            return taken + kept

        lax.fori_loop(0, blocks, step, jnp.int32(0))


def slot_tables(masks, capacity):
    row_blocks, blocks = masks.shape
    smem = pl.BlockSpec(memory_space=pltpu.SMEM)
    return pl.pallas_call(
        tables_kernel,
        out_shape=(
            jax.ShapeDtypeStruct((row_blocks, capacity), jnp.int32),
            jax.ShapeDtypeStruct((row_blocks, capacity), jnp.int32),
            jax.ShapeDtypeStruct((row_blocks, blocks), jnp.int32),
        ),
        in_specs=[smem],
        out_specs=(smem, smem, smem),
    )(masks)


def rows_kernel(count, tok_ref, cot_ref, tok_all, cot_all, send_sem, recv_sem, own_sem):
    me = lax.axis_index("tp")
    barrier = pltpu.get_barrier_semaphore()
    for shift in range(1, count):
        pl.semaphore_signal(
            barrier, inc=1, device_id={"tp": lax.rem(me + shift, count)}, device_id_type=MESH
        )
    pl.semaphore_wait(barrier, count - 1)
    copies = []
    for which, (src, dst) in enumerate(((tok_ref, tok_all), (cot_ref, cot_all))):
        for shift in range(1, count):
            copy = pltpu.make_async_remote_copy(
                src_ref=src,
                dst_ref=dst.at[me],
                send_sem=send_sem.at[which, shift],
                recv_sem=recv_sem.at[which, shift],
                device_id={"tp": lax.rem(me + shift, count)},
                device_id_type=MESH,
            )
            copy.start()
            copies.append(copy)
        own = pltpu.make_async_copy(src, dst.at[me], own_sem.at[which])
        own.start()
        copies.append(own)
    for copy in copies:
        copy.wait()


def gather_rows(tokens, cotangent):
    count = lax.axis_size("tp")
    rows, feats = tokens.shape
    anywhere = pl.BlockSpec(memory_space=pl.ANY)
    return pl.pallas_call(
        functools.partial(rows_kernel, count),
        out_shape=(jax.ShapeDtypeStruct((count, rows, feats), tokens.dtype),) * 2,
        in_specs=[anywhere] * 2,
        out_specs=(anywhere,) * 2,
        scratch_shapes=[
            pltpu.SemaphoreType.DMA((2, count)),
            pltpu.SemaphoreType.DMA((2, count)),
            pltpu.SemaphoreType.DMA((2,)),
        ],
        compiler_params=pltpu.CompilerParams(collective_id=0, has_side_effects=True),
    )(tokens, cotangent)


def parts_kernel(group, block_ref, live_ref, tok_ref, cot_ref, *refs):
    gates, ups, downs = refs[:group], refs[group : 2 * group], refs[2 * group : 3 * group]
    out_ref = refs[3 * group]
    row, step = pl.program_id(0), pl.program_id(1)
    tok, cot = tok_ref[...], cot_ref[...]
    owners, _, own_rows, _ = out_ref.shape
    for at in range(group):
        live = live_ref[row, step * group + at] == 1
        columns = slice(at * BLK, (at + 1) * BLK)
        gate = jnp.dot(tok, gates[at][...], preferred_element_type=jnp.float32)
        up = jnp.dot(tok, ups[at][...], preferred_element_type=jnp.float32)
        grad = lax.dot_general(
            cot, downs[at][...], (((1,), (1,)), ((), ())), preferred_element_type=jnp.float32
        )
        up = jnp.where(live, up, 0.0)
        grad = jnp.where(live, grad, 0.0)
        for which, value in enumerate((gate, up, grad)):
            out_ref[:, which, :, columns] = value.reshape(owners, own_rows, BLK)


def weight_specs(group, feats):
    def columns(at):
        return pl.BlockSpec(
            (feats, BLK), lambda row, step, block, live: (0, block[row, step * group + at])
        )

    def rows(at):
        return pl.BlockSpec(
            (BLK, feats), lambda row, step, block, live: (block[row, step * group + at], 0)
        )

    return (
        [columns(at) for at in range(group)] * 2 + [rows(at) for at in range(group)]
    )


def partial_products(block, live, tok, cot, gate_w, up_w, down_w, own_rows):
    row_blocks, capacity = block.shape
    feats = tok.shape[1]
    group = group_of(capacity)
    owners = ROWBLK // own_rows
    rows_spec = pl.BlockSpec((ROWBLK, feats), lambda row, step, block, live: (row, 0))
    flops = 6 * row_blocks * ROWBLK * feats * capacity * BLK
    return pl.pallas_call(
        functools.partial(parts_kernel, group),
        out_shape=jax.ShapeDtypeStruct(
            (row_blocks * owners, 3, own_rows, capacity * BLK), jnp.float32
        ),
        grid_spec=pltpu.PrefetchScalarGridSpec(
            num_scalar_prefetch=2,
            grid=(row_blocks, capacity // group),
            in_specs=[rows_spec, rows_spec] + weight_specs(group, feats),
            out_specs=pl.BlockSpec(
                (owners, 3, own_rows, group * BLK), lambda row, step, block, live: (row, 0, 0, step)
            ),
        ),
        compiler_params=pltpu.CompilerParams(vmem_limit_bytes=VMEM_LIMIT),
        cost_estimate=pl.CostEstimate(
            flops=flops, bytes_accessed=flops // ROWBLK, transcendentals=0
        ),
    )(block, live, tok, cot, *([gate_w] * group + [up_w] * group + [down_w] * group))


def exchange_kernel(
    count, part_ref, all_ref, paired, summed, landed, acts,
    pair_send, pair_recv, sum_send, sum_recv, side_send, up_send, down_send, all_recv,
    hand_send, hand_recv, own_sem,
):
    chips = count // 2
    me = lax.axis_index("seq")
    chip, core = me // 2, lax.rem(me, 2)
    sibling = me + 1 - 2 * core
    tall = 4 if chips % 4 == 0 else chips
    wide = chips // tall
    along, across = chip // wide, lax.rem(chip, wide)
    columns = part_ref.shape[3]
    piece = group_of(columns // BLK) * BLK
    halves = 2 if columns // piece % 2 == 0 else 1
    width = columns // halves

    def ahead(shift):
        return lax.rem(chip + shift, chips)

    barrier = pltpu.get_barrier_semaphore()
    pl.semaphore_signal(barrier, inc=1, device_id={"seq": sibling}, device_id_type=MESH)
    for shift in range(1, chips):
        pl.semaphore_signal(
            barrier, inc=1, device_id={"seq": ahead(shift) * 2 + core}, device_id_type=MESH
        )
    pl.semaphore_wait(barrier, chips)

    def pair_copy(shift):
        return pltpu.make_async_remote_copy(
            src_ref=part_ref.at[ahead(shift) * 2 + 1 - core],
            dst_ref=paired.at[shift],
            send_sem=pair_send.at[shift],
            recv_sem=pair_recv.at[shift],
            device_id={"seq": sibling},
            device_id_type=MESH,
        )

    def part_of(half):
        return slice(half * width, (half + 1) * width)

    def sum_copy(half, shift):
        return pltpu.make_async_remote_copy(
            src_ref=summed.at[shift, :, :, part_of(half)],
            dst_ref=landed.at[shift, :, :, part_of(half)],
            send_sem=sum_send.at[half, shift],
            recv_sem=sum_recv.at[half, shift],
            device_id={"seq": ahead(shift) * 2 + core},
            device_id_type=MESH,
        )

    def route(half, owner, dest, send, src=None):
        slot = all_ref.at[owner * 2 + core, :, :, part_of(half)]
        return pltpu.make_async_remote_copy(
            src_ref=slot if src is None else src,
            dst_ref=slot,
            send_sem=send.at[half, owner],
            recv_sem=all_recv.at[half, owner],
            device_id={"seq": dest * 2 + core},
            device_id_type=MESH,
        )

    def hand_copy(half, owner, side, src=None):
        slot = all_ref.at[owner * 2 + side, :, :, part_of(half)]
        return pltpu.make_async_remote_copy(
            src_ref=slot if src is None else src,
            dst_ref=slot,
            send_sem=hand_send.at[half, owner],
            recv_sem=hand_recv.at[half, owner],
            device_id={"seq": sibling},
            device_id_type=MESH,
        )

    for shift in list(range(1, chips)) + [0]:
        pair_copy(shift).start()

    def send_sum(half, shift, carry):
        if half == 0:
            pair_copy(shift).wait_recv()
        mine = ahead(shift) * 2 + core
        for which in range(3):
            for start in range(half * width, (half + 1) * width, piece):
                cut = slice(start, start + piece)
                summed[shift, which, :, cut] = (
                    part_ref[mine, which, :, cut] + paired[shift, which, :, cut]
                ).astype(jnp.bfloat16)
        sum_copy(half, shift).start()
        return carry

    for half in range(halves):
        lax.fori_loop(1, chips, functools.partial(send_sum, half), 0)
    pair_copy(0).wait_recv()

    def arrived(half, shift, carry):
        sum_copy(half, shift).wait_recv()
        return carry

    def act(step, carry):
        cut = pl.ds(pl.multiple_of(step * piece, BLK), piece)

        def total(which):
            value = part_ref[me, which, :, cut] + paired[0, which, :, cut]
            for shift in range(1, chips):
                value = value + landed[shift, which, :, cut].astype(jnp.float32)
            return value

        gate, up, grad = total(0), total(1), total(2)
        sig = jax.nn.sigmoid(gate)
        acts[0, :, cut] = (gate * sig * up).astype(jnp.bfloat16)
        acts[1, :, cut] = (grad * up * sig * (1.0 + gate * (1.0 - sig))).astype(jnp.bfloat16)
        acts[2, :, cut] = (grad * gate * sig).astype(jnp.bfloat16)
        return carry

    def aside(step):
        return lax.rem(across + step, wide)

    def pass_on(half, owner, up, down, src=None):
        @pl.when(jnp.logical_and(up, along < tall - 1))
        def _():
            route(half, owner, chip + wide, up_send, src).start()

        @pl.when(jnp.logical_and(down, along > 0))
        def _():
            route(half, owner, chip - wide, down_send, src).start()

        hand_copy(half, owner, core, src).start()

    def take(half, owner):
        route(half, owner, chip, up_send).wait_recv()

    for half in range(halves):
        lax.fori_loop(1, chips, functools.partial(arrived, half), 0)
        steps = width // piece
        lax.fori_loop(half * steps, (half + 1) * steps, act, 0)

        own = pltpu.make_async_copy(acts.at[:, :, part_of(half)], all_ref.at[me, :, :, part_of(half)], own_sem.at[half])
        own.start()

        yes, no = jnp.bool_(True), jnp.bool_(False)
        for step in range(1, wide):
            pltpu.make_async_remote_copy(
                src_ref=acts.at[:, :, part_of(half)],
                dst_ref=all_ref.at[me, :, :, part_of(half)],
                send_sem=side_send.at[half, step],
                recv_sem=all_recv.at[half, chip],
                device_id={"seq": (along * wide + aside(step)) * 2 + core},
                device_id_type=MESH,
            ).start()
        pass_on(half, chip, yes, yes, acts.at[:, :, part_of(half)])
        for step in range(1, wide):
            owner = along * wide + aside(step)
            take(half, owner)
            pass_on(half, owner, yes, yes)
        for far in range(1, tall):
            for step in range(wide):

                @pl.when(along >= far)
                def _():
                    owner = (along - far) * wide + aside(step)
                    take(half, owner)
                    pass_on(half, owner, yes, no)

                @pl.when(along + far < tall)
                def _():
                    owner = (along + far) * wide + aside(step)
                    take(half, owner)
                    pass_on(half, owner, no, yes)

    for half in range(halves):
        pltpu.make_async_copy(acts.at[:, :, part_of(half)], all_ref.at[me, :, :, part_of(half)], own_sem.at[half]).wait()
        for step in range(1, wide):
            pltpu.make_async_remote_copy(
                src_ref=acts.at[:, :, part_of(half)],
                dst_ref=all_ref.at[me, :, :, part_of(half)],
                send_sem=side_send.at[half, step],
                recv_sem=all_recv.at[half, chip],
                device_id={"seq": (along * wide + aside(step)) * 2 + core},
                device_id_type=MESH,
            ).wait_send()

        def finish(owner, carry):
            hand_copy(half, owner, 1 - core).wait_recv()
            hand_copy(half, owner, core).wait_send()
            if half == 0:
                pair_copy(owner).wait_send()

            @pl.when(jnp.logical_and(owner // wide <= along, along < tall - 1))
            def _():
                route(half, owner, chip + wide, up_send).wait_send()

            @pl.when(jnp.logical_and(owner // wide >= along, along > 0))
            def _():
                route(half, owner, chip - wide, down_send).wait_send()

            return carry

        lax.fori_loop(0, chips, finish, 0)

        def sent(shift, carry):
            sum_copy(half, shift).wait_send()
            return carry

        lax.fori_loop(1, chips, sent, 0)


def exchange(parts):
    count = lax.axis_size("seq")
    chips = count // 2
    chunk = parts.shape[1:]
    pair = [pltpu.SemaphoreType.DMA((chips,))] * 2
    sems = pair + [pltpu.SemaphoreType.DMA((2, chips))] * 8
    return pl.pallas_call(
        functools.partial(exchange_kernel, count),
        out_shape=jax.ShapeDtypeStruct(parts.shape, jnp.bfloat16),
        in_specs=[pl.BlockSpec(memory_space=pltpu.VMEM)],
        out_specs=pl.BlockSpec(memory_space=pl.ANY),
        scratch_shapes=[
            pltpu.VMEM((chips,) + chunk, jnp.float32),
            pltpu.VMEM((chips,) + chunk, jnp.bfloat16),
            pltpu.VMEM((chips,) + chunk, jnp.bfloat16),
            pltpu.VMEM(chunk, jnp.bfloat16),
        ]
        + sems
        + [pltpu.SemaphoreType.DMA((2,))],
        compiler_params=pltpu.CompilerParams(
            collective_id=1, has_side_effects=True, vmem_limit_bytes=VMEM_LIMIT
        ),
    )(parts)


def rows_out_kernel(group, block_ref, live_ref, act_ref, *refs):
    gates, ups, downs = refs[:group], refs[group : 2 * group], refs[2 * group : 3 * group]
    out_ref = refs[3 * group]
    step = pl.program_id(1)

    @pl.when(step == 0)
    def _():
        out_ref[...] = jnp.zeros_like(out_ref)

    out = jnp.zeros(out_ref.shape[2:], jnp.float32)
    grad = jnp.zeros(out_ref.shape[2:], jnp.float32)
    across = (((1,), (1,)), ((), ()))
    for at in range(group):
        columns = slice(at * BLK, (at + 1) * BLK)
        hid, dgate, dup = (act_ref[:, which, :, columns].reshape(ROWBLK, BLK) for which in range(3))
        out += jnp.dot(hid, downs[at][...], preferred_element_type=jnp.float32)
        grad += lax.dot_general(dgate, gates[at][...], across, preferred_element_type=jnp.float32)
        grad += lax.dot_general(dup, ups[at][...], across, preferred_element_type=jnp.float32)
    out_ref[0, 0] += out
    out_ref[0, 1] += grad


def rows_out(block, live, acts, gate_w, up_w, down_w):
    row_blocks, capacity = block.shape
    own_rows = acts.shape[2]
    feats = gate_w.shape[0]
    group = group_of(capacity)
    owners = ROWBLK // own_rows
    flops = 6 * row_blocks * ROWBLK * feats * capacity * BLK
    return pl.pallas_call(
        functools.partial(rows_out_kernel, group),
        out_shape=jax.ShapeDtypeStruct((row_blocks, 2, ROWBLK, feats), jnp.float32),
        grid_spec=pltpu.PrefetchScalarGridSpec(
            num_scalar_prefetch=2,
            grid=(row_blocks, capacity // group),
            in_specs=[
                pl.BlockSpec(
                    (owners, 3, own_rows, group * BLK),
                    lambda row, step, block, live: (row, 0, 0, step),
                )
            ]
            + weight_specs(group, feats),
            out_specs=pl.BlockSpec(
                (1, 2, ROWBLK, feats), lambda row, step, block, live: (row, 0, 0, 0)
            ),
        ),
        compiler_params=pltpu.CompilerParams(vmem_limit_bytes=VMEM_LIMIT),
        cost_estimate=pl.CostEstimate(
            flops=flops, bytes_accessed=flops // ROWBLK, transcendentals=0
        ),
    )(block, live, acts, *([gate_w] * group + [up_w] * group + [down_w] * group))


def weights_out_kernel(
    group, scale, slot_ref, mask_ref, tok_ref, cot_ref, act_ref, gate_ref, up_ref, down_ref,
    flipped, dense,
):
    step = pl.program_id(0)
    row_blocks = mask_ref.shape[0]
    owners = ROWBLK // act_ref.shape[2]

    @pl.when(step == 0)
    def _():
        flipped[...] = tok_ref[...].T

    for at in range(group):
        for row in range(row_blocks):
            kept = mask_ref[row, step * group + at] == 1
            slot = pl.ds(pl.multiple_of(slot_ref[row, step * group + at] * BLK, BLK), BLK)
            for which in range(3):
                value = act_ref[row * owners : (row + 1) * owners, which, :, slot]
                value = jnp.where(kept, value, jnp.zeros_like(value))
                dense[which, row * ROWBLK : (row + 1) * ROWBLK, at * BLK : (at + 1) * BLK] = (
                    value.reshape(ROWBLK, BLK)
                )
    tok = flipped[...]
    gate_ref[...] = jnp.dot(tok, dense[1], preferred_element_type=jnp.float32) * scale
    up_ref[...] = jnp.dot(tok, dense[2], preferred_element_type=jnp.float32) * scale
    down_ref[...] = (
        lax.dot_general(
            dense[0], cot_ref[...], (((0,), (0,)), ((), ())), preferred_element_type=jnp.float32
        )
        * scale
    )


def weights_out(slots, masks, tok, cot, acts):
    row_blocks, blocks = masks.shape
    rows, feats = tok.shape
    group = group_of(blocks)
    whole = pl.BlockSpec((rows, feats), lambda step, slot, mask: (0, 0))
    wide = pl.BlockSpec((feats, group * BLK), lambda step, slot, mask: (0, step))
    hidden = blocks * BLK
    return pl.pallas_call(
        functools.partial(weights_out_kernel, group, 1.0 / math.sqrt(rows)),
        out_shape=(
            jax.ShapeDtypeStruct((feats, hidden), jnp.float32),
            jax.ShapeDtypeStruct((feats, hidden), jnp.float32),
            jax.ShapeDtypeStruct((hidden, feats), jnp.float32),
        ),
        grid_spec=pltpu.PrefetchScalarGridSpec(
            num_scalar_prefetch=2,
            grid=(blocks // group,),
            in_specs=[
                whole,
                whole,
                pl.BlockSpec(acts.shape, lambda step, slot, mask: (0, 0, 0, 0)),
            ],
            out_specs=(
                wide,
                wide,
                pl.BlockSpec((group * BLK, feats), lambda step, slot, mask: (step, 0)),
            ),
            scratch_shapes=[
                pltpu.VMEM((feats, rows), jnp.bfloat16),
                pltpu.VMEM((3, rows, group * BLK), jnp.bfloat16),
            ],
        ),
        compiler_params=pltpu.CompilerParams(vmem_limit_bytes=VMEM_LIMIT),
        cost_estimate=pl.CostEstimate(
            flops=6 * rows * feats * hidden, bytes_accessed=12 * feats * hidden, transcendentals=0
        ),
    )(slots, masks, tok, cot, acts)


def shards(tokens, gate_weight, up_weight, down_weight, masks, cotangent):
    seq_count = lax.axis_size("seq")
    tp_count = lax.axis_size("tp")
    rank = lax.axis_index("tp")
    rows, feats = tokens.shape
    total_rows = rows * tp_count
    kept_total = masks.shape[1] * tp_count // KEEP_PART
    capacity = min(2 * kept_total // tp_count, masks.shape[1])
    tok, cot = (value.reshape(total_rows, feats) for value in gather_rows(tokens, cotangent))
    block, live, slots = slot_tables(masks, capacity)
    parts = partial_products(
        block, live, tok, cot, gate_weight, up_weight, down_weight, total_rows // seq_count
    )
    acts = exchange(parts)
    row_parts = rows_out(block, live, acts, gate_weight, up_weight, down_weight)
    row_parts = jnp.swapaxes(row_parts.reshape(tp_count, rows // ROWBLK, 2, ROWBLK, feats), 1, 2)
    moved = []
    for shift in range(1, tp_count):
        piece = lax.dynamic_index_in_dim(
            row_parts, lax.rem(rank + shift, tp_count), 0, keepdims=False
        ).astype(jnp.bfloat16)
        pairs = [(src, (src + shift) % tp_count) for src in range(tp_count)]
        moved.append(lax.ppermute(piece, "tp", pairs))
    grad_gate, grad_up, grad_down = weights_out(slots, masks, tok, cot, acts)
    mine = lax.dynamic_index_in_dim(row_parts, rank, 0, keepdims=False)
    for piece in moved:
        mine = mine + piece.astype(jnp.float32)
    mine = mine.reshape(2, rows, feats).astype(jnp.bfloat16)
    return (mine[0], mine[1], grad_gate, grad_up, grad_down)


def solution(mesh):
    placed = (
        P("tp", "seq"),
        P("seq", "tp"),
        P("seq", "tp"),
        P("tp", "seq"),
        P(None, "tp"),
        P("tp", "seq"),
    )
    return jax.shard_map(
        shards,
        mesh=mesh,
        in_specs=placed,
        out_specs=(P("tp", "seq"), P("tp", "seq"), P("seq", "tp"), P("seq", "tp"), P("tp", "seq")),
        check_vma=False,
    )
```
